128 devices in a mesh: row: 8 (over y_lo, x), col: 16 (over z, y_hi, core).
Axes of the slice: x: 4, y: 4 (y_hi: 2, y_lo: 2; y = y_hi * 2 + y_lo), z: 4, core: 2. Of those that a mesh axis runs over, the one named last changes fastest.
Arguments:
- sources: bfloat16 [64, 32768], P(None, ('row', 'col')), may hold values from -6 to 6
- near_tiles: bfloat16 [128, 128, 256, 256], P('row', 'col'), may hold values from -0.03125 to 0.03125
- far_left: bfloat16 [128, 128, 32, 256], P('row', 'col'), may hold values from -1 to 1
- far_right: bfloat16 [128, 128, 32, 256], P('row', 'col'), may hold values from -0.03125 to 0.03125
- pattern: int32 [128, 128], P('row', 'col'), may hold values from 0 to 2
- band_end: int32 [128], P('row'), may hold values from 0 to 127, as said below
Outputs:
- image: float32 [64, 32768], P(None, ('row', 'col'))
The draws below stay inside these ranges and needn't reach their ends.
Inputs may be any that keep to these rules, and one draw needn't show every extreme that they name: band_end[I] is at least I, so the band of every block-row starts at its own cluster; the bands of block-rows 0 to 15 run to the last cluster.
All inputs are finite; a program needn't handle non-finite values.
Results may differ from the reference program's by a relative error of at most 0.0021.
Values may be sent and summed in bfloat16 or wider, within the bound.
A program may use at most 128 MiB of HBM per device.

```python
import jax
import jax.numpy as jnp
from jax import lax

CASES = 64
BS = 256
RANK = 32
NC = 128
PANELS = 32768
N_ROW = 8
N_COL = 16


def draw_band_end(key, part):
    row_ids = jnp.arange(NC, dtype=jnp.int32)
    reach = jax.random.randint(jax.random.fold_in(key, 17), (NC,), NC // 4, NC // 2 + 1, dtype=jnp.int32)
    banded = jnp.minimum(row_ids + reach, NC - 1).astype(jnp.int32)
    return jnp.where(row_ids < N_COL, NC - 1, banded).astype(jnp.int32)


def plant(values, rng, least, largest):
    extent = values.shape
    index_at = [jax.random.randint(jax.random.fold_in(rng, axis), (), 0, extent[axis]) for axis in range(len(extent))]
    values = values.at[tuple(index_at)].set(least)
    longest = extent.index(max(extent))
    index_at[longest] = (index_at[longest] + 1) % extent[longest]
    return values.at[tuple(index_at)].set(largest)


def levels(stream_key, dims, pieces, least, high):
    gain = 1.0
    for axis_at, shards_of in pieces:
        heights = jax.random.uniform(jax.random.fold_in(jax.random.fold_in(stream_key, 6), axis_at), (shards_of,), jnp.float32, least / len(pieces), high / len(pieces))
        gain = gain * jnp.repeat(jnp.exp(heights), dims[axis_at] // shards_of).reshape((-1,) + (1,) * (len(dims) - 1 - axis_at))
    return gain


def bell_draw(key, dims, spread, most, cuts=(), held_as=jnp.bfloat16):
    factor_of = levels(key, dims, cuts, -0.22, 0.18) if cuts else 1.0
    values = jax.random.normal(key, dims, jnp.float32) * spread * factor_of
    return jnp.minimum(jnp.maximum(values, -most), most).astype(held_as)


def setup_inputs(seed: int = 0) -> dict:
    splits = jax.random.split(jax.random.key(seed), 7)
    return {
        "sources": bell_draw(splits[0], (CASES, PANELS), 1.0, 6.0, ((1, 128),)),
        "near_tiles": bell_draw(splits[1], (NC, NC, BS, BS), (BS * NC) ** -0.5, 0.03125, ((0, 8), (1, 16))),
        "far_left": bell_draw(splits[2], (NC, NC, RANK, BS), RANK ** -0.5, 1.0, ((0, 8), (1, 16))),
        "far_right": bell_draw(splits[3], (NC, NC, RANK, BS), (BS * NC) ** -0.5, 0.03125, ((0, 8), (1, 16))),
        "pattern": plant(jax.random.randint(splits[4], (NC, NC), 0, 3), jax.random.fold_in(splits[4], 1), 0, 2).astype(jnp.int32),
        "band_end": draw_band_end(jax.random.fold_in(splits[6], 71), 0),
    }


def rounded(values):
    low = lax.optimization_barrier(values.astype(jnp.bfloat16))
    return low.astype(jnp.float32)


def reference(sources, near_tiles, far_left, far_right, pattern, band_end):
    num_cases = sources.shape[0]
    clusters = sources.reshape(num_cases, NC, BS).transpose(1, 0, 2).astype(jnp.float32)
    slots = jnp.arange(NC, dtype=jnp.int32)
    col_ids = ((slots % N_ROW) * N_COL + slots // N_ROW).astype(jnp.int32)
    ordered = clusters[col_ids]

    def one_row(carry, inputs):
        row_id, tiles, left, right, kinds, limit = inputs
        live = (row_id <= col_ids) & (col_ids <= limit)
        near_mask = jnp.where(live & (kinds == 1), 1.0, 0.0).astype(jnp.float32)
        far_mask = jnp.where(live & (kinds == 2), 1.0, 0.0).astype(jnp.float32)
        tiles_wide = tiles.astype(jnp.float32)
        left_wide = left.astype(jnp.float32)
        right_wide = right.astype(jnp.float32)
        near_rows = jnp.einsum("qab,qcb->qca", tiles_wide, ordered)
        far_coef = rounded(jnp.einsum("qrb,qcb->qcr", right_wide, ordered))
        far_rows = jnp.einsum("qra,qcr->qca", left_wide, far_coef)
        row_out = jnp.einsum("q,qca->ca", near_mask, near_rows) + jnp.einsum("q,qca->ca", far_mask, far_rows)
        own = lax.dynamic_index_in_dim(clusters, row_id, 0, keepdims=False)
        near_cols = jnp.einsum("qab,ca->qcb", tiles_wide, own)
        back_coef = rounded(jnp.einsum("qra,ca->qcr", left_wide, own))
        far_cols = jnp.einsum("qrb,qcr->qcb", right_wide, back_coef)
        contrib = near_mask[:, None, None] * near_cols + far_mask[:, None, None] * far_cols
        carry = carry.at[col_ids].add(contrib)
        return carry, row_out

    start = jnp.zeros((NC, num_cases, BS), jnp.float32)
    carry, rows = lax.scan(one_row, start, (jnp.arange(NC, dtype=jnp.int32), near_tiles, far_left, far_right, pattern, band_end))
    total = rows + carry
    return total.transpose(1, 0, 2).reshape(num_cases, NC * BS)
```

```python
import functools

import jax
import jax.numpy as jnp
from jax import lax
from jax.experimental import pallas as pl
from jax.experimental.pallas import tpu as pltpu
from jax.sharding import PartitionSpec as P

MESH = pl.DeviceIdType.MESH
F32 = jnp.float32
BF16 = jnp.bfloat16
LANES = 128


def dot_nt(a, b):
    return lax.dot_general(a, b, (((1,), (1,)), ((), ())), preferred_element_type=F32)


def dot_nn(a, b):
    return lax.dot_general(a, b, (((1,), (0,)), ((), ())), preferred_element_type=F32)


def kernel(
    src_hbm, near_hbm, left_hbm, right_hbm, pat_ref, band_ref, out_ref,
    tiles, left, right, own, row_src, col_src, fwd, bwd, row_send, row_recv, col_send, col_recv,
    own_sem, near_sem, far_sem, gr_send, gr_recv, gc_send, gc_recv, rr_send, rr_recv, rc_send, rc_recv,
):
    n_row, n_col = near_hbm.shape[1], near_hbm.shape[0]
    rank = left_hbm.shape[2]
    per = LANES // rank
    row, col = lax.axis_index("row"), lax.axis_index("col")

    own_copy = pltpu.make_async_copy(src_hbm, own, own_sem)
    own_copy.start()
    right_copy = pltpu.make_async_copy(right_hbm, right, far_sem.at[0])
    left_copy = pltpu.make_async_copy(left_hbm, left, far_sem.at[1])
    right_copy.start()
    left_copy.start()

    def near_copy(i):
        return pltpu.make_async_copy(near_hbm.at[i], tiles.at[i], near_sem.at[i])

    for i in range(n_col):
        near_copy(i).start()

    barrier = pltpu.get_barrier_semaphore()

    @pl.loop(1, n_col)
    def _(d):
        pl.semaphore_signal(
            barrier, inc=1, device_id={"col": lax.rem(col + d, n_col)}, device_id_type=MESH
        )

    @pl.loop(1, n_row)
    def _(d):
        pl.semaphore_signal(
            barrier, inc=1, device_id={"row": lax.rem(row + d, n_row)}, device_id_type=MESH
        )

    pl.semaphore_wait(barrier, n_col + n_row - 2)

    def to_row(k, src, dst, send, recv):
        return pltpu.make_async_remote_copy(
            src_ref=src, dst_ref=dst, send_sem=send, recv_sem=recv,
            device_id={"row": k}, device_id_type=MESH,
        )

    def to_col(c, src, dst, send, recv):
        return pltpu.make_async_remote_copy(
            src_ref=src, dst_ref=dst, send_sem=send, recv_sem=recv,
            device_id={"col": c}, device_id_type=MESH,
        )

    own_copy.wait()

    @pl.loop(0, row)
    def _(k):
        to_row(k, own, col_src.at[row], gc_send.at[k], gc_recv.at[row]).start()

    @pl.loop(1, n_col)
    def _(d):
        c = lax.rem(col + d, n_col)
        to_col(c, own, row_src.at[col], gr_send.at[c], gr_recv.at[col]).start()

    col_src[row] = own[...]
    row_src[col] = own[...]

    @pl.loop(0, row)
    def _(k):
        col_src[k] = jnp.zeros_like(own)

    def weight(i, k, kind):
        big_i, big_j = row * n_col + i, k * n_col + col
        ok = (big_i <= big_j) & (big_j <= band_ref[i]) & (pat_ref[i, k] == kind)
        return jnp.where(ok, 1.0, 0.0).astype(F32)

    lane = lax.broadcasted_iota(jnp.int32, (1, LANES), 1) // rank
    num_cases = own.shape[0]
    wide_lane = lax.broadcasted_iota(jnp.int32, (num_cases, LANES), 1) // rank

    def lay(parts, place):
        total = parts[-1]
        for p in range(per - 1):
            total = jnp.where(place == p, parts[p], total)
        return total

    @pl.loop(row + 1, n_row)
    def _(k):
        to_row(row, own, col_src.at[k], gc_send.at[row], gc_recv.at[k]).wait_recv()

    right_copy.wait()
    pairs = n_col // per // 2

    @pl.loop(0, n_row // per)
    def _(kk):
        @pl.loop(0, pairs)
        def _(gp):
            coef = []
            for s in range(per):
                k = kk * per + s
                rows = [
                    right[(gp * 2 + g) * per + (p - s) % per, k] for g in range(2) for p in range(per)
                ]
                coef.append(dot_nt(col_src[k], jnp.concatenate(rows, axis=0)))
            for g in range(2):
                for t in range(per):
                    i = (gp * 2 + g) * per + t
                    piece = lay(
                        [coef[(p - t) % per][:, g * LANES:(g + 1) * LANES] for p in range(per)],
                        wide_lane,
                    )
                    keep = lay(
                        [jnp.full((1, LANES), weight(i, kk * per + (p - t) % per, 2), F32) for p in range(per)],
                        lane,
                    )
                    fwd[i, kk] = (piece * keep).astype(BF16)

    left_copy.wait()

    def left_rows(i):
        return jnp.concatenate(
            [
                left[i, kk * per + lax.rem(p - i + n_col, per)]
                for kk in range(n_row // per)
                for p in range(per)
            ],
            axis=0,
        )

    @pl.loop(0, n_col)
    def _(i):
        near_copy(i).wait()
        acc = dot_nn(
            jnp.concatenate([fwd[i, kk] for kk in range(n_row // per)], axis=1), left_rows(i)
        )
        for k in range(n_row):
            acc += dot_nt(col_src[k] * weight(i, k, 1).astype(BF16), tiles[i, k])

        @pl.when(i == col)
        def _():
            out_ref[...] = acc

        @pl.when(i != col)
        def _():
            row_send[i] = acc.astype(BF16)
            to_col(i, row_send.at[i], row_recv.at[col], rr_send.at[i], rr_recv.at[col]).start()

    @pl.loop(1, n_col)
    def _(d):
        c = lax.rem(col + d, n_col)
        to_col(col, own, row_src.at[c], gr_send.at[col], gr_recv.at[c]).wait_recv()

    @pl.loop(0, n_col // per)
    def _(g):
        back = [dot_nt(row_src[g * per + t], left_rows(g * per + t)) for t in range(per)]
        for kk in range(n_row // per):
            for s in range(per):
                k = kk * per + s
                piece = lay(
                    [back[(p - s) % per][:, kk * LANES:(kk + 1) * LANES] for p in range(per)],
                    wide_lane,
                )
                keep = lay(
                    [jnp.full((1, LANES), weight(g * per + (p - s) % per, k, 2), F32) for p in range(per)],
                    lane,
                )
                bwd[k, g] = (piece * keep).astype(BF16)

    @pl.loop(0, n_row - row)
    def _(step):
        k = n_row - 1 - step
        acc = jnp.zeros((num_cases, own.shape[1]), F32)
        for h in range(n_col // per // 2):
            rows = [
                right[(h * 2 + g) * per + lax.rem(p - k + n_row, per), k]
                for g in range(2)
                for p in range(per)
            ]
            acc += dot_nn(
                jnp.concatenate([bwd[k, h * 2], bwd[k, h * 2 + 1]], axis=1),
                jnp.concatenate(rows, axis=0),
            )
        for i in range(n_col):
            acc += dot_nn(row_src[i] * weight(i, k, 1).astype(BF16), tiles[i, k])

        @pl.when(k == row)
        def _():
            out_ref[...] += acc

        @pl.when(k != row)
        def _():
            col_send[k] = acc.astype(BF16)
            to_row(k, col_send.at[k], col_recv.at[row], rc_send.at[k], rc_recv.at[row]).start()

    @pl.loop(1, n_col)
    def _(d):
        c = lax.rem(col + d, n_col)
        to_col(col, own, row_recv.at[c], rr_send.at[col], rr_recv.at[c]).wait_recv()
        out_ref[...] += row_recv[c].astype(F32)

    @pl.loop(0, row)
    def _(k):
        to_row(row, own, col_recv.at[k], rc_send.at[row], rc_recv.at[k]).wait_recv()
        out_ref[...] += col_recv[k].astype(F32)

    @pl.loop(1, n_col)
    def _(d):
        c = lax.rem(col + d, n_col)
        to_col(c, own, row_src.at[col], gr_send.at[c], gr_recv.at[col]).wait_send()
        to_col(c, row_send.at[c], row_recv.at[col], rr_send.at[c], rr_recv.at[col]).wait_send()

    @pl.loop(0, row)
    def _(k):
        to_row(k, own, col_src.at[row], gc_send.at[k], gc_recv.at[row]).wait_send()

    @pl.loop(row + 1, n_row)
    def _(k):
        to_row(k, col_send.at[k], col_recv.at[row], rc_send.at[k], rc_recv.at[row]).wait_send()


def shards(sources, near_tiles, far_left, far_right, pattern, band_end):
    n_col, n_row, size = near_tiles.shape[:3]
    rank = far_left.shape[2]
    cases = sources.shape[0]
    per = LANES // rank
    dma = pltpu.SemaphoreType.DMA
    hbm = pl.BlockSpec(memory_space=pltpu.HBM)
    smem = pl.BlockSpec(memory_space=pltpu.SMEM)
    return pl.pallas_call(
        kernel,
        out_shape=jax.ShapeDtypeStruct((cases, size), F32),
        in_specs=[hbm, hbm, hbm, hbm, smem, smem],
        out_specs=pl.BlockSpec(memory_space=pltpu.VMEM),
        scratch_shapes=[
            pltpu.VMEM(near_tiles.shape, BF16),
            pltpu.VMEM(far_left.shape, BF16),
            pltpu.VMEM(far_right.shape, BF16),
            pltpu.VMEM((cases, size), BF16),
            pltpu.VMEM((n_col, cases, size), BF16),
            pltpu.VMEM((n_row, cases, size), BF16),
            pltpu.VMEM((n_col, n_row // per, cases, LANES), BF16),
            pltpu.VMEM((n_row, n_col // per, cases, LANES), BF16),
            pltpu.VMEM((n_col, cases, size), BF16),
            pltpu.VMEM((n_col, cases, size), BF16),
            pltpu.VMEM((n_row, cases, size), BF16),
            pltpu.VMEM((n_row, cases, size), BF16),
            dma,
            dma((n_col,)),
            dma((2,)),
            dma((n_col,)), dma((n_col,)),
            dma((n_row,)), dma((n_row,)),
            dma((n_col,)), dma((n_col,)),
            dma((n_row,)), dma((n_row,)),
        ],
        compiler_params=pltpu.CompilerParams(
            collective_id=0, has_side_effects=True, vmem_limit_bytes=40 * 1024 * 1024
        ),
        name="panels",
    )(sources, near_tiles, far_left, far_right, pattern, band_end)


def solution(mesh):
    placed = (
        P(None, ("row", "col")),
        P("row", "col", None, None),
        P("row", "col", None, None),
        P("row", "col", None, None),
        P("row", "col"),
        P("row"),
    )
    return jax.shard_map(
        shards, mesh=mesh, in_specs=placed, out_specs=P(None, ("row", "col")), check_vma=False
    )
```

```python
import functools

import jax
import jax.numpy as jnp
from jax import lax
from jax.experimental import pallas as pl
from jax.experimental.pallas import tpu as pltpu
from jax.sharding import PartitionSpec as P

MESH = pl.DeviceIdType.MESH
F32 = jnp.float32
BF16 = jnp.bfloat16
LANES = 128


def dot_nt(a, b):
    return lax.dot_general(a, b, (((1,), (1,)), ((), ())), preferred_element_type=F32)


def dot_nn(a, b):
    return lax.dot_general(a, b, (((1,), (0,)), ((), ())), preferred_element_type=F32)


def kernel(
    src_hbm, near_hbm, left_hbm, right_hbm, pat_ref, band_ref, out_ref,
    tiles, turned, left, right, own, row_src, col_src, fwd, bwd, fwd_keep, bwd_keep, near_keep,
    pair_send, pair_recv, row_send, row_recv, col_send, col_recv,
    own_sem, near_sem, far_sem, gr_send, gr_recv, gc_send, gc_recv,
    pa_send, pa_recv, rr_send, rr_recv, rc_send, rc_recv,
):
    n_row, n_col = near_hbm.shape[1], near_hbm.shape[0]
    rank = left_hbm.shape[2]
    num_cases, size = own.shape
    per = LANES // rank
    chips = n_col // 2
    planes = n_col // 4
    row, col = lax.axis_index("row"), lax.axis_index("col")
    core, chip = lax.rem(col, 2), col // 2
    partner = col + 1 - 2 * core

    def other(c, d):
        return lax.rem(c + 2 * d, n_col)

    barrier = pltpu.get_barrier_semaphore()

    def greet(device):
        pl.semaphore_signal(barrier, inc=1, device_id=device, device_id_type=MESH)

    for d in range(1, n_row):
        greet({"row": lax.rem(row + d, n_row)})
    for d in range(1, chips):
        greet({"col": other(col, d)})
    greet({"col": partner})

    own_copy = pltpu.make_async_copy(src_hbm, own, own_sem)
    own_copy.start()
    right_copy = pltpu.make_async_copy(right_hbm, right, far_sem.at[0])
    left_copy = pltpu.make_async_copy(left_hbm, left, far_sem.at[1])
    right_copy.start()
    left_copy.start()

    def near_copy(i):
        return pltpu.make_async_copy(near_hbm.at[i], tiles.at[i], near_sem.at[i])

    def theirs(t):
        return 2 * t + 1 - core

    def ours(s):
        q = s // 2
        dz = jnp.where(q == 0, 2, jnp.where(q == 1, 1, jnp.where(q == 2, 3, 0)))
        dy = 1 - lax.rem(s, 2)
        z, y = chip // 2, lax.rem(chip, 2)
        return lax.rem(z + dz, planes) * 2 + lax.rem(y + dy, 2)

    @pl.loop(0, chips)
    def _(t):
        near_copy(theirs(t)).start()

    @pl.loop(0, chips)
    def _(s):
        near_copy(2 * ours(s) + core).start()

    pl.semaphore_wait(barrier, n_row - 1 + chips)

    def to_row(k, src, dst, send, recv):
        return pltpu.make_async_remote_copy(
            src_ref=src, dst_ref=dst, send_sem=send, recv_sem=recv,
            device_id={"row": k}, device_id_type=MESH,
        )

    def to_col(c, src, dst, send, recv):
        return pltpu.make_async_remote_copy(
            src_ref=src, dst_ref=dst, send_sem=send, recv_sem=recv,
            device_id={"col": c}, device_id_type=MESH,
        )

    def give(block, origin, device, slot):
        return to_col(device, block, row_src.at[origin], gr_send.at[slot], gr_recv.at[origin])

    def got(origin):
        give(own, origin, partner, 0).wait_recv()

    own_copy.wait()

    @pl.loop(0, row)
    def _(k):
        to_row(k, own, col_src.at[row], gc_send.at[k], gc_recv.at[row]).start()

    @pl.loop(1, chips)
    def _(d):
        give(own, col, other(col, d), d).start()

    give(own, col, partner, 0).start()

    col_src[row] = own[...]
    row_src[col] = own[...]

    @pl.loop(0, row)
    def _(k):
        col_src[k] = jnp.zeros_like(own)

    def weight(i, k, kind):
        big_i, big_j = row * n_col + i, k * n_col + col
        ok = (big_i <= big_j) & (big_j <= band_ref[i]) & (pat_ref[k, i] == kind)
        return jnp.where(ok, 1.0, 0.0).astype(F32)

    lane = lax.broadcasted_iota(jnp.int32, (1, LANES), 1) // rank
    wide_lane = lax.broadcasted_iota(jnp.int32, (num_cases, LANES), 1) // rank

    def lay(parts, place):
        total = parts[-1]
        for p in range(per - 1):
            total = jnp.where(place == p, parts[p], total)
        return total

    @pl.loop(0, n_col // per)
    def _(g):
        for kk in range(n_row // per):
            far = {}
            for t in range(per):
                for s in range(per):
                    i, k = g * per + t, kk * per + s
                    far[t, s] = jnp.full((1, LANES), weight(i, k, 2), F32)
                    near_keep[i * n_row + k] = weight(i, k, 1)
            for t in range(per):
                fwd_keep[g * per + t, kk] = lay([far[t, (p - t) % per] for p in range(per)], lane)
            for s in range(per):
                bwd_keep[kk * per + s, g] = lay([far[(p - s) % per, s] for p in range(per)], lane)

    def turn(i):
        near_copy(i).wait()
        for k in range(n_row):
            turned[i, k] = tiles[i, k].T

    @pl.loop(0, chips)
    def _(t):
        turn(theirs(t))

    @pl.loop(0, chips)
    def _(s):
        turn(2 * ours(s) + core)

    @pl.loop(row + 1, n_row)
    def _(k):
        to_row(row, own, col_src.at[k], gc_send.at[row], gc_recv.at[k]).wait_recv()

    right_copy.wait()
    for kk in range(n_row // per):
        for gp in range(n_col // per // 2):
            coef = []
            for s in range(per):
                k = kk * per + s
                rows = [
                    right[(gp * 2 + g) * per + (p - s) % per, k] for g in range(2) for p in range(per)
                ]
                coef.append(dot_nt(col_src[k], jnp.concatenate(rows, axis=0)))
            for g in range(2):
                for t in range(per):
                    i = (gp * 2 + g) * per + t
                    piece = lay(
                        [coef[(p - t) % per][:, g * LANES:(g + 1) * LANES] for p in range(per)],
                        wide_lane,
                    )
                    fwd[i, kk] = (piece * fwd_keep[i, kk]).astype(BF16)

    @pl.loop(1, chips)
    def _(d):
        origin = other(col, d)
        got(origin)
        give(row_src.at[origin], origin, partner, chips - 1 + d).start()

    left_copy.wait()

    def left_rows(i):
        return jnp.concatenate(
            [
                left[i, kk * per + lax.rem(p - i + n_col, per)]
                for kk in range(n_row // per)
                for p in range(per)
            ],
            axis=0,
        )

    def row_term(i):
        acc = dot_nn(
            jnp.concatenate([fwd[i, kk] for kk in range(n_row // per)], axis=1), left_rows(i)
        )
        for k in range(n_row):
            acc += dot_nn(col_src[k] * near_keep[i * n_row + k].astype(BF16), turned[i, k])
        return acc

    def pair_copy(t):
        return to_col(partner, pair_send.at[t], pair_recv.at[t], pa_send.at[t], pa_recv.at[t])

    def row_copy(t):
        return to_col(
            2 * t + core, row_send.at[t], row_recv.at[chip], rr_send.at[t], rr_recv.at[chip]
        )

    @pl.loop(0, chips // 2)
    def _(h):
        terms = [row_term(theirs(2 * h + u)) for u in range(2)]
        for u in range(2):
            pair_send[2 * h + u] = terms[u]
        for u in range(2):
            pair_copy(2 * h + u).start()

    @pl.loop(0, chips // 2)
    def _(h):
        terms = [row_term(2 * ours(2 * h + u) + core) for u in range(2)]
        for u in range(2):
            t = ours(2 * h + u)
            pair_copy(t).wait_recv()
            acc = terms[u] + pair_recv[t]

            @pl.when(t == chip)
            def _():
                out_ref[...] = acc

            @pl.when(t != chip)
            def _():
                row_send[t] = acc.astype(BF16)
                row_copy(t).start()

    @pl.loop(0, chips)
    def _(d):
        got(other(partner, d))

    for g in range(n_col // per):
        back = [dot_nt(row_src[g * per + t], left_rows(g * per + t)) for t in range(per)]
        for kk in range(n_row // per):
            for s in range(per):
                k = kk * per + s
                piece = lay(
                    [back[(p - s) % per][:, kk * LANES:(kk + 1) * LANES] for p in range(per)],
                    wide_lane,
                )
                bwd[k, g] = (piece * bwd_keep[k, g]).astype(BF16)

    def col_copy(k):
        return to_row(k, col_send.at[k], col_recv.at[row], rc_send.at[k], rc_recv.at[row])

    def col_term(k):
        acc = jnp.zeros((num_cases, size), F32)
        for h in range(n_col // per // 2):
            rows = [
                right[(h * 2 + g) * per + lax.rem(p - k + n_row, per), k]
                for g in range(2)
                for p in range(per)
            ]
            acc += dot_nn(
                jnp.concatenate([bwd[k, h * 2], bwd[k, h * 2 + 1]], axis=1),
                jnp.concatenate(rows, axis=0),
            )
        for i in range(n_col):
            acc += dot_nn(row_src[i] * near_keep[i * n_row + k].astype(BF16), tiles[i, k])
        return acc

    @pl.loop(0, n_row // 2)
    def _(step):
        high = n_row - 1 - 2 * step

        @pl.when(high >= row)
        def _():
            terms = [col_term(high - u) for u in range(2)]
            for u in range(2):
                k, acc = high - u, terms[u]

                @pl.when(k == row)
                def _():
                    out_ref[...] += acc

                @pl.when(k > row)
                def _():
                    col_send[k] = acc.astype(BF16)
                    col_copy(k).start()

    @pl.loop(1, chips)
    def _(d):
        t = lax.rem(chip + d, chips)
        to_col(col, own, row_recv.at[t], rr_send.at[chip], rr_recv.at[t]).wait_recv()
        out_ref[...] += row_recv[t].astype(F32)

    @pl.loop(0, row)
    def _(k):
        to_row(row, own, col_recv.at[k], rc_send.at[row], rc_recv.at[k]).wait_recv()
        out_ref[...] += col_recv[k].astype(F32)

    @pl.loop(0, n_col - 1)
    def _(slot):
        give(own, col, partner, slot).wait_send()

    @pl.loop(0, chips)
    def _(t):
        pair_copy(t).wait_send()

    @pl.loop(1, chips)
    def _(d):
        row_copy(lax.rem(chip + d, chips)).wait_send()

    @pl.loop(0, row)
    def _(k):
        to_row(k, own, col_src.at[row], gc_send.at[k], gc_recv.at[row]).wait_send()

    @pl.loop(row + 1, n_row)
    def _(k):
        col_copy(k).wait_send()


def shards(sources, near_tiles, far_left, far_right, pattern, band_end):
    n_col, n_row, size = near_tiles.shape[:3]
    rank = far_left.shape[2]
    cases = sources.shape[0]
    per = LANES // rank
    dma = pltpu.SemaphoreType.DMA
    hbm = pl.BlockSpec(memory_space=pltpu.HBM)
    smem = pl.BlockSpec(memory_space=pltpu.SMEM)
    return pl.pallas_call(
        kernel,
        out_shape=jax.ShapeDtypeStruct((cases, size), F32),
        in_specs=[hbm, hbm, hbm, hbm, smem, smem],
        out_specs=pl.BlockSpec(memory_space=pltpu.VMEM),
        scratch_shapes=[
            pltpu.VMEM(near_tiles.shape, BF16),
            pltpu.VMEM(near_tiles.shape, BF16),
            pltpu.VMEM(far_left.shape, BF16),
            pltpu.VMEM(far_right.shape, BF16),
            pltpu.VMEM((cases, size), BF16),
            pltpu.VMEM((n_col, cases, size), BF16),
            pltpu.VMEM((n_row, cases, size), BF16),
            pltpu.VMEM((n_col, n_row // per, cases, LANES), BF16),
            pltpu.VMEM((n_row, n_col // per, cases, LANES), BF16),
            pltpu.VMEM((n_col, n_row // per, 1, LANES), F32),
            pltpu.VMEM((n_row, n_col // per, 1, LANES), F32),
            pltpu.SMEM((n_col * n_row,), F32),
            pltpu.VMEM((n_col // 2, cases, size), F32),
            pltpu.VMEM((n_col // 2, cases, size), F32),
            pltpu.VMEM((n_col // 2, cases, size), BF16),
            pltpu.VMEM((n_col // 2, cases, size), BF16),
            pltpu.VMEM((n_row, cases, size), BF16),
            pltpu.VMEM((n_row, cases, size), BF16),
            dma,
            dma((n_col,)),
            dma((2,)),
            dma((n_col - 1,)), dma((n_col,)),
            dma((n_row,)), dma((n_row,)),
            dma((n_col // 2,)), dma((n_col // 2,)),
            dma((n_col // 2,)), dma((n_col // 2,)),
            dma((n_row,)), dma((n_row,)),
        ],
        compiler_params=pltpu.CompilerParams(
            collective_id=0, has_side_effects=True, vmem_limit_bytes=60 * 1024 * 1024
        ),
        name="panels",
    )(sources, near_tiles, far_left, far_right, pattern.T, band_end)


def solution(mesh):
    placed = (
        P(None, ("row", "col")),
        P("row", "col", None, None),
        P("row", "col", None, None),
        P("row", "col", None, None),
        P("row", "col"),
        P("row"),
    )
    return jax.shard_map(
        shards, mesh=mesh, in_specs=placed, out_specs=P(None, ("row", "col")), check_vma=False
    )
```

```python
import functools

import jax
import jax.numpy as jnp
from jax import lax
from jax.experimental import pallas as pl
from jax.experimental.pallas import tpu as pltpu
from jax.sharding import PartitionSpec as P

MESH = pl.DeviceIdType.MESH
F32 = jnp.float32
BF16 = jnp.bfloat16
LANES = 128


def dot_nt(a, b):
    return lax.dot_general(a, b, (((1,), (1,)), ((), ())), preferred_element_type=F32)


def dot_nn(a, b):
    return lax.dot_general(a, b, (((1,), (0,)), ((), ())), preferred_element_type=F32)


def kernel(
    src_hbm, near_hbm, left_hbm, right_hbm, pat_ref, band_ref, out_ref,
    tiles, turned, left, right, own, row_src, col_src, fwd, bwd, fwd_keep, bwd_keep, near_keep,
    pair_send, pair_recv, row_send, row_recv, col_send, col_recv,
    own_sem, near_sem, far_sem, gr_send, gr_recv, gc_send, gc_recv,
    pa_send, pa_recv, rr_send, rr_recv, rc_send, rc_recv,
):
    n_row, n_col = near_hbm.shape[2], 2 * near_hbm.shape[0]
    rank = left_hbm.shape[2]
    num_cases, size = own.shape
    per = LANES // rank
    chips = n_col // 2
    planes = n_col // 4
    row, col = lax.axis_index("row"), lax.axis_index("col")
    core, chip = lax.rem(col, 2), col // 2
    partner = col + 1 - 2 * core

    def other(c, d):
        return lax.rem(c + 2 * d, n_col)

    own_copy = pltpu.make_async_copy(src_hbm, own, own_sem)
    own_copy.start()

    barrier = pltpu.get_barrier_semaphore()

    def greet(device):
        pl.semaphore_signal(barrier, inc=1, device_id=device, device_id_type=MESH)

    for d in range(1, chips):
        greet({"col": other(col, d)})
    for d in range(1, n_row):
        greet({"row": lax.rem(row + d, n_row)})
    greet({"col": partner})

    right_copy = pltpu.make_async_copy(right_hbm, right, far_sem.at[0])
    left_copy = pltpu.make_async_copy(left_hbm, left, far_sem.at[1])
    right_copy.start()
    left_copy.start()

    quarter = chips // 2

    def near_copy(side, part):
        span = pl.ds(part * quarter, quarter)
        return pltpu.make_async_copy(
            near_hbm.at[span, side], tiles.at[span, side], near_sem.at[side, part]
        )

    def theirs(t):
        return 2 * t + 1 - core

    def ours(s):
        q = s // 2
        dz = jnp.where(q == 0, 2, jnp.where(q == 1, 1, jnp.where(q == 2, 3, 0)))
        dy = 1 - lax.rem(s, 2)
        z, y = chip // 2, lax.rem(chip, 2)
        return lax.rem(z + dz, planes) * 2 + lax.rem(y + dy, 2)

    for side in (1 - core, core):
        for part in range(2):
            near_copy(side, part).start()

    pl.semaphore_wait(barrier, n_row - 1 + chips)

    def to_row(k, src, dst, send, recv):
        return pltpu.make_async_remote_copy(
            src_ref=src, dst_ref=dst, send_sem=send, recv_sem=recv,
            device_id={"row": k}, device_id_type=MESH,
        )

    def to_col(c, src, dst, send, recv):
        return pltpu.make_async_remote_copy(
            src_ref=src, dst_ref=dst, send_sem=send, recv_sem=recv,
            device_id={"col": c}, device_id_type=MESH,
        )

    def give(block, origin, device, slot):
        return to_col(device, block, row_src.at[origin], gr_send.at[slot], gr_recv.at[origin])

    def got(origin):
        give(own, origin, partner, 0).wait_recv()

    own_copy.wait()

    @pl.loop(0, row)
    def _(k):
        to_row(k, own, col_src.at[row], gc_send.at[k], gc_recv.at[row]).start()

    @pl.loop(1, chips)
    def _(d):
        give(own, col, other(col, d), d).start()

    give(own, col, partner, 0).start()

    col_src[row] = own[...]
    row_src[col] = own[...]

    @pl.loop(0, row)
    def _(k):
        col_src[k] = jnp.zeros_like(own)

    def weight(i, k, kind):
        big_i, big_j = row * n_col + i, k * n_col + col
        ok = (big_i <= big_j) & (big_j <= band_ref[i]) & (pat_ref[k, i] == kind)
        return jnp.where(ok, 1.0, 0.0).astype(F32)

    lane = lax.broadcasted_iota(jnp.int32, (1, LANES), 1) // rank
    wide_lane = lax.broadcasted_iota(jnp.int32, (num_cases, LANES), 1) // rank

    def lay(parts, place):
        total = parts[-1]
        for p in range(per - 1):
            total = jnp.where(place == p, parts[p], total)
        return total

    @pl.loop(0, n_col // per)
    def _(g):
        for kk in range(n_row // per):
            far = {}
            for t in range(per):
                for s in range(per):
                    i, k = g * per + t, kk * per + s
                    far[t, s] = jnp.full((1, LANES), weight(i, k, 2), F32)
                    near_keep[i * n_row + k] = weight(i, k, 1)
            for t in range(per):
                fwd_keep[g * per + t, kk] = lay([far[t, (p - t) % per] for p in range(per)], lane)
            for s in range(per):
                bwd_keep[kk * per + s, g] = lay([far[(p - s) % per, s] for p in range(per)], lane)

    def turn(t, side):
        for k in range(n_row):
            turned[t, side, k] = tiles[t, side, k].T

    for part in range(2):
        near_copy(1 - core, part).wait()

        @pl.loop(part * quarter, (part + 1) * quarter)
        def _(t):
            turn(t, 1 - core)

    for part in range(2):
        near_copy(core, part).wait()

    @pl.loop(0, quarter)
    def _(s):
        turn(ours(s), core)

    @pl.loop(row + 1, n_row)
    def _(k):
        to_row(row, own, col_src.at[k], gc_send.at[row], gc_recv.at[k]).wait_recv()

    right_copy.wait()
    for kk in range(n_row // per):
        for gp in range(n_col // per // 2):
            coef = []
            for s in range(per):
                k = kk * per + s
                rows = [
                    right[(gp * 2 + g) * per + (p - s) % per, k] for g in range(2) for p in range(per)
                ]
                coef.append(dot_nt(col_src[k], jnp.concatenate(rows, axis=0)))
            for g in range(2):
                for t in range(per):
                    i = (gp * 2 + g) * per + t
                    piece = lay(
                        [coef[(p - t) % per][:, g * LANES:(g + 1) * LANES] for p in range(per)],
                        wide_lane,
                    )
                    fwd[i, kk] = (piece * fwd_keep[i, kk]).astype(BF16)

    @pl.loop(1, chips)
    def _(d):
        origin = other(col, d)
        got(origin)
        give(row_src.at[origin], origin, partner, chips - 1 + d).start()

    left_copy.wait()

    def left_rows(i):
        return jnp.concatenate(
            [
                left[i, kk * per + lax.rem(p - i + n_col, per)]
                for kk in range(n_row // per)
                for p in range(per)
            ],
            axis=0,
        )

    def row_term(i):
        acc = dot_nn(
            jnp.concatenate([fwd[i, kk] for kk in range(n_row // per)], axis=1), left_rows(i)
        )
        for k in range(n_row):
            acc += dot_nn(col_src[k] * near_keep[i * n_row + k].astype(BF16), turned[i // 2, lax.rem(i, 2), k])
        return acc

    def pair_copy(t):
        return to_col(partner, pair_send.at[t], pair_recv.at[t], pa_send.at[t], pa_recv.at[t])

    def row_copy(t):
        return to_col(
            2 * t + core, row_send.at[t], row_recv.at[chip], rr_send.at[t], rr_recv.at[chip]
        )

    @pl.loop(0, chips // 2)
    def _(h):
        terms = [row_term(theirs(2 * h + u)) for u in range(2)]
        turn(ours(quarter + h), core)
        for u in range(2):
            pair_send[2 * h + u] = terms[u]
        for u in range(2):
            pair_copy(2 * h + u).start()

    @pl.loop(0, chips // 2)
    def _(h):
        terms = [row_term(2 * ours(2 * h + u) + core) for u in range(2)]
        for u in range(2):
            t = ours(2 * h + u)
            pair_copy(t).wait_recv()
            acc = terms[u] + pair_recv[t]

            @pl.when(t == chip)
            def _():
                out_ref[...] = acc

            @pl.when(t != chip)
            def _():
                row_send[t] = acc.astype(BF16)
                row_copy(t).start()

    @pl.loop(0, chips)
    def _(d):
        got(other(partner, d))

    for g in range(n_col // per):
        back = [dot_nt(row_src[g * per + t], left_rows(g * per + t)) for t in range(per)]
        for kk in range(n_row // per):
            for s in range(per):
                k = kk * per + s
                piece = lay(
                    [back[(p - s) % per][:, kk * LANES:(kk + 1) * LANES] for p in range(per)],
                    wide_lane,
                )
                bwd[k, g] = (piece * bwd_keep[k, g]).astype(BF16)

    def col_copy(k):
        return to_row(k, col_send.at[k], col_recv.at[row], rc_send.at[k], rc_recv.at[row])

    def col_term(k):
        acc = jnp.zeros((num_cases, size), F32)
        for h in range(n_col // per // 2):
            rows = [
                right[(h * 2 + g) * per + lax.rem(p - k + n_row, per), k]
                for g in range(2)
                for p in range(per)
            ]
            acc += dot_nn(
                jnp.concatenate([bwd[k, h * 2], bwd[k, h * 2 + 1]], axis=1),
                jnp.concatenate(rows, axis=0),
            )
        for i in range(n_col):
            acc += dot_nn(row_src[i] * near_keep[i * n_row + k].astype(BF16), tiles[i // 2, i % 2, k])
        return acc

    @pl.loop(0, n_row // 2)
    def _(step):
        high = n_row - 1 - 2 * step

        @pl.when(high >= row)
        def _():
            terms = [col_term(high - u) for u in range(2)]
            for u in range(2):
                k, acc = high - u, terms[u]

                @pl.when(k == row)
                def _():
                    out_ref[...] += acc

                @pl.when(k > row)
                def _():
                    col_send[k] = acc.astype(BF16)
                    col_copy(k).start()

    @pl.loop(1, chips)
    def _(d):
        t = lax.rem(chip + d, chips)
        to_col(col, own, row_recv.at[t], rr_send.at[chip], rr_recv.at[t]).wait_recv()
        out_ref[...] += row_recv[t].astype(F32)

    @pl.loop(0, row)
    def _(k):
        last = row - 1 - k
        to_row(row, own, col_recv.at[last], rc_send.at[row], rc_recv.at[last]).wait_recv()
        out_ref[...] += col_recv[last].astype(F32)

    @pl.loop(0, n_col - 1)
    def _(slot):
        give(own, col, partner, slot).wait_send()

    @pl.loop(0, chips)
    def _(t):
        pair_copy(t).wait_send()

    @pl.loop(1, chips)
    def _(d):
        row_copy(lax.rem(chip + d, chips)).wait_send()

    @pl.loop(0, row)
    def _(k):
        to_row(k, own, col_src.at[row], gc_send.at[k], gc_recv.at[row]).wait_send()

    @pl.loop(row + 1, n_row)
    def _(k):
        col_copy(k).wait_send()


def shards(sources, near_tiles, far_left, far_right, pattern, band_end):
    n_col, n_row, size = near_tiles.shape[:3]
    rank = far_left.shape[2]
    cases = sources.shape[0]
    per = LANES // rank
    pairs = near_tiles.reshape(n_col // 2, 2, n_row, size, size)
    dma = pltpu.SemaphoreType.DMA
    hbm = pl.BlockSpec(memory_space=pltpu.HBM)
    smem = pl.BlockSpec(memory_space=pltpu.SMEM)
    return pl.pallas_call(
        kernel,
        out_shape=jax.ShapeDtypeStruct((cases, size), F32),
        in_specs=[hbm, hbm, hbm, hbm, smem, smem],
        out_specs=pl.BlockSpec(memory_space=pltpu.VMEM),
        scratch_shapes=[
            pltpu.VMEM(pairs.shape, BF16),
            pltpu.VMEM(pairs.shape, BF16),
            pltpu.VMEM(far_left.shape, BF16),
            pltpu.VMEM(far_right.shape, BF16),
            pltpu.VMEM((cases, size), BF16),
            pltpu.VMEM((n_col, cases, size), BF16),
            pltpu.VMEM((n_row, cases, size), BF16),
            pltpu.VMEM((n_col, n_row // per, cases, LANES), BF16),
            pltpu.VMEM((n_row, n_col // per, cases, LANES), BF16),
            pltpu.VMEM((n_col, n_row // per, 1, LANES), F32),
            pltpu.VMEM((n_row, n_col // per, 1, LANES), F32),
            pltpu.SMEM((n_col * n_row,), F32),
            pltpu.VMEM((n_col // 2, cases, size), F32),
            pltpu.VMEM((n_col // 2, cases, size), F32),
            pltpu.VMEM((n_col // 2, cases, size), BF16),
            pltpu.VMEM((n_col // 2, cases, size), BF16),
            pltpu.VMEM((n_row, cases, size), BF16),
            pltpu.VMEM((n_row, cases, size), BF16),
            dma,
            dma((2, 2)),
            dma((2,)),
            dma((n_col - 1,)), dma((n_col,)),
            dma((n_row,)), dma((n_row,)),
            dma((n_col // 2,)), dma((n_col // 2,)),
            dma((n_col // 2,)), dma((n_col // 2,)),
            dma((n_row,)), dma((n_row,)),
        ],
        compiler_params=pltpu.CompilerParams(
            collective_id=0, has_side_effects=True, vmem_limit_bytes=60 * 1024 * 1024
        ),
        name="panels",
    )(sources, pairs, far_left, far_right, pattern.T, band_end)


def solution(mesh):
    placed = (
        P(None, ("row", "col")),
        P("row", "col", None, None),
        P("row", "col", None, None),
        P("row", "col", None, None),
        P("row", "col"),
        P("row"),
    )
    return jax.shard_map(
        shards, mesh=mesh, in_specs=placed, out_specs=P(None, ("row", "col")), check_vma=False
    )
```

```python
import functools

import jax
import jax.numpy as jnp
from jax import lax
from jax.experimental import pallas as pl
from jax.experimental.pallas import tpu as pltpu
from jax.sharding import PartitionSpec as P

MESH = pl.DeviceIdType.MESH
F32 = jnp.float32
BF16 = jnp.bfloat16
LANES = 128


def dot_nt(a, b):
    return lax.dot_general(a, b, (((1,), (1,)), ((), ())), preferred_element_type=F32)


def dot_nn(a, b):
    return lax.dot_general(a, b, (((1,), (0,)), ((), ())), preferred_element_type=F32)


def kernel(
    src_hbm, near_hbm, left_hbm, right_hbm, pat_ref, band_ref, out_ref,
    tiles, turned, left, right, own, row_src, col_src, fwd, bwd, fwd_keep, bwd_keep, near_keep,
    pair_send, pair_recv, row_send, row_recv, col_send, col_recv,
    row_open, col_open, own_sem, near_sem, far_sem, gr_send, gr_recv, gc_send, gc_recv,
    pa_send, pa_recv, rr_send, rr_recv, rc_send, rc_recv,
):
    n_row, n_col = near_hbm.shape[2], 2 * near_hbm.shape[0]
    rank = left_hbm.shape[2]
    num_cases, size = own.shape
    per = LANES // rank
    chips = n_col // 2
    planes = n_col // 4
    row, col = lax.axis_index("row"), lax.axis_index("col")
    core, chip = lax.rem(col, 2), col // 2
    partner = col + 1 - 2 * core

    def other(c, d):
        return lax.rem(c + 2 * d, n_col)

    own_copy = pltpu.make_async_copy(src_hbm, own, own_sem)
    own_copy.start()

    barrier = pltpu.get_barrier_semaphore()

    def greet(device):
        pl.semaphore_signal(barrier, inc=1, device_id=device, device_id_type=MESH)

    @pl.loop(row + 1, n_row)
    def _(k):
        greet({"row": k, "col": col - core})

    @pl.when(core == 1)
    def _():
        greet({"col": partner})

    for d in range(1, chips):
        greet({"col": other(col - core + 1, d)})

    right_copy = pltpu.make_async_copy(right_hbm, right, far_sem.at[0])
    left_copy = pltpu.make_async_copy(left_hbm, left, far_sem.at[1])

    quarter = chips // 2

    def near_copy(side, part):
        span = pl.ds(part * quarter, quarter)
        return pltpu.make_async_copy(
            near_hbm.at[span, side], tiles.at[span, side], near_sem.at[side, part]
        )

    def theirs(t):
        return 2 * t + 1 - core

    def ours(s):
        q = s // 2
        dz = jnp.where(q == 0, 2, jnp.where(q == 1, 1, jnp.where(q == 2, 3, 0)))
        dy = 1 - lax.rem(s, 2)
        z, y = chip // 2, lax.rem(chip, 2)
        return lax.rem(z + dz, planes) * 2 + lax.rem(y + dy, 2)

    first = 1 - core
    for side in (first, core):
        for part in range(2):
            near_copy(side, part).start()
            if side is first and part == 0:
                right_copy.start()
                left_copy.start()

    @pl.when(core == 0)
    def _():
        pl.semaphore_wait(barrier, 2 * row + 1)
        pl.semaphore_signal(row_open, inc=1, device_id={"col": partner}, device_id_type=MESH)

    @pl.when(core == 1)
    def _():
        pl.semaphore_wait(row_open, 1)

    def to_row(k, src, dst, send, recv):
        return pltpu.make_async_remote_copy(
            src_ref=src, dst_ref=dst, send_sem=send, recv_sem=recv,
            device_id={"row": k}, device_id_type=MESH,
        )

    def to_col(c, src, dst, send, recv):
        return pltpu.make_async_remote_copy(
            src_ref=src, dst_ref=dst, send_sem=send, recv_sem=recv,
            device_id={"col": c}, device_id_type=MESH,
        )

    def give(block, origin, device, slot):
        return to_col(device, block, row_src.at[origin], gr_send.at[slot], gr_recv.at[origin])

    def got(origin):
        give(own, origin, partner, 0).wait_recv()

    own_copy.wait()

    @pl.loop(0, row)
    def _(k):
        to_row(k, own, col_src.at[row], gc_send.at[k], gc_recv.at[row]).start()

    give(own, col, partner, 0).start()

    col_src[row] = own[...]
    row_src[col] = own[...]

    @pl.loop(0, row)
    def _(k):
        col_src[k] = jnp.zeros_like(own)

    def weight(i, k, kind):
        big_i, big_j = row * n_col + i, k * n_col + col
        ok = (big_i <= big_j) & (big_j <= band_ref[i]) & (pat_ref[k, i] == kind)
        return jnp.where(ok, 1.0, 0.0).astype(F32)

    lane = lax.broadcasted_iota(jnp.int32, (1, LANES), 1) // rank
    wide_lane = lax.broadcasted_iota(jnp.int32, (num_cases, LANES), 1) // rank

    def lay(parts, place):
        total = parts[-1]
        for p in range(per - 1):
            total = jnp.where(place == p, parts[p], total)
        return total

    @pl.loop(0, n_col // per)
    def _(g):
        for kk in range(n_row // per):
            far = {}
            for t in range(per):
                for s in range(per):
                    i, k = g * per + t, kk * per + s
                    far[t, s] = jnp.full((1, LANES), weight(i, k, 2), F32)
                    near_keep[i * n_row + k] = weight(i, k, 1)
            for t in range(per):
                fwd_keep[g * per + t, kk] = lay([far[t, (p - t) % per] for p in range(per)], lane)
            for s in range(per):
                bwd_keep[kk * per + s, g] = lay([far[(p - s) % per, s] for p in range(per)], lane)

    def turn(t, side):
        for k in range(n_row):
            turned[t, side, k] = tiles[t, side, k].T

    near_copy(1 - core, 0).wait()

    @pl.loop(0, quarter)
    def _(t):
        turn(t, 1 - core)

    @pl.when(core == 1)
    def _():
        pl.semaphore_wait(barrier, 2 * (chips - 1))
        pl.semaphore_signal(col_open, inc=1, device_id={"col": partner}, device_id_type=MESH)

    @pl.when(core == 0)
    def _():
        pl.semaphore_wait(col_open, 1)

    @pl.loop(1, chips)
    def _(d):
        give(own, col, other(col, d), d).start()

    for part in range(1, 2):
        near_copy(1 - core, part).wait()

        @pl.loop(part * quarter, (part + 1) * quarter)
        def _(t):
            turn(t, 1 - core)

    for part in range(2):
        near_copy(core, part).wait()

    @pl.loop(0, quarter)
    def _(s):
        turn(ours(s), core)

    @pl.loop(row + 1, n_row)
    def _(k):
        to_row(row, own, col_src.at[k], gc_send.at[row], gc_recv.at[k]).wait_recv()

    right_copy.wait()
    for kk in range(n_row // per):
        for gp in range(n_col // per // 2):
            coef = []
            for s in range(per):
                k = kk * per + s
                rows = [
                    right[(gp * 2 + g) * per + (p - s) % per, k] for g in range(2) for p in range(per)
                ]
                coef.append(dot_nt(col_src[k], jnp.concatenate(rows, axis=0)))
            for g in range(2):
                for t in range(per):
                    i = (gp * 2 + g) * per + t
                    piece = lay(
                        [coef[(p - t) % per][:, g * LANES:(g + 1) * LANES] for p in range(per)],
                        wide_lane,
                    )
                    fwd[i, kk] = (piece * fwd_keep[i, kk]).astype(BF16)

    left_copy.wait()

    def left_rows(i):
        return jnp.concatenate(
            [
                left[i, kk * per + lax.rem(p - i + n_col, per)]
                for kk in range(n_row // per)
                for p in range(per)
            ],
            axis=0,
        )

    def row_term(i):
        acc = dot_nn(
            jnp.concatenate([fwd[i, kk] for kk in range(n_row // per)], axis=1), left_rows(i)
        )
        for k in range(n_row):
            acc += dot_nn(col_src[k] * near_keep[i * n_row + k].astype(BF16), turned[i // 2, lax.rem(i, 2), k])
        return acc

    def pair_copy(t):
        return to_col(partner, pair_send.at[t], pair_recv.at[t], pa_send.at[t], pa_recv.at[t])

    def row_copy(t):
        return to_col(
            2 * t + core, row_send.at[t], row_recv.at[chip], rr_send.at[t], rr_recv.at[chip]
        )

    @pl.loop(0, chips // 2)
    def _(h):
        terms = [row_term(theirs(2 * h + u)) for u in range(2)]
        turn(ours(quarter + h), core)
        for u in range(2):
            pair_send[2 * h + u] = terms[u]
        for u in range(2):
            pair_copy(2 * h + u).start()

    @pl.loop(1, chips)
    def _(d):
        origin = other(col, d)
        got(origin)
        give(row_src.at[origin], origin, partner, chips - 1 + d).start()

    @pl.loop(0, chips // 2)
    def _(h):
        terms = [row_term(2 * ours(2 * h + u) + core) for u in range(2)]
        for u in range(2):
            t = ours(2 * h + u)
            pair_copy(t).wait_recv()
            acc = terms[u] + pair_recv[t]

            @pl.when(t == chip)
            def _():
                out_ref[...] = acc

            @pl.when(t != chip)
            def _():
                row_send[t] = acc.astype(BF16)
                row_copy(t).start()

    @pl.loop(0, chips)
    def _(d):
        got(other(partner, d))

    for g in range(n_col // per):
        back = [dot_nt(row_src[g * per + t], left_rows(g * per + t)) for t in range(per)]
        for kk in range(n_row // per):
            for s in range(per):
                k = kk * per + s
                piece = lay(
                    [back[(p - s) % per][:, kk * LANES:(kk + 1) * LANES] for p in range(per)],
                    wide_lane,
                )
                bwd[k, g] = (piece * bwd_keep[k, g]).astype(BF16)

    def col_copy(k):
        return to_row(k, col_send.at[k], col_recv.at[row], rc_send.at[k], rc_recv.at[row])

    def col_term(k):
        acc = jnp.zeros((num_cases, size), F32)
        for h in range(n_col // per // 2):
            rows = [
                right[(h * 2 + g) * per + lax.rem(p - k + n_row, per), k]
                for g in range(2)
                for p in range(per)
            ]
            acc += dot_nn(
                jnp.concatenate([bwd[k, h * 2], bwd[k, h * 2 + 1]], axis=1),
                jnp.concatenate(rows, axis=0),
            )
        for i in range(n_col):
            acc += dot_nn(row_src[i] * near_keep[i * n_row + k].astype(BF16), tiles[i // 2, i % 2, k])
        return acc

    @pl.loop(0, n_row // 2)
    def _(step):
        high = n_row - 1 - 2 * step

        @pl.when(high >= row)
        def _():
            terms = [col_term(high - u) for u in range(2)]
            for u in range(2):
                k, acc = high - u, terms[u]

                @pl.when(k == row)
                def _():
                    out_ref[...] += acc

                @pl.when(k > row)
                def _():
                    col_send[k] = acc.astype(BF16)
                    col_copy(k).start()

    @pl.loop(1, chips)
    def _(d):
        t = lax.rem(chip + d, chips)
        to_col(col, own, row_recv.at[t], rr_send.at[chip], rr_recv.at[t]).wait_recv()
        out_ref[...] += row_recv[t].astype(F32)

    @pl.loop(0, row)
    def _(k):
        last = row - 1 - k
        to_row(row, own, col_recv.at[last], rc_send.at[row], rc_recv.at[last]).wait_recv()
        out_ref[...] += col_recv[last].astype(F32)

    @pl.loop(0, n_col - 1)
    def _(slot):
        give(own, col, partner, slot).wait_send()

    @pl.loop(0, chips)
    def _(t):
        pair_copy(t).wait_send()

    @pl.loop(1, chips)
    def _(d):
        row_copy(lax.rem(chip + d, chips)).wait_send()

    @pl.loop(0, row)
    def _(k):
        to_row(k, own, col_src.at[row], gc_send.at[k], gc_recv.at[row]).wait_send()

    @pl.loop(row + 1, n_row)
    def _(k):
        col_copy(k).wait_send()


def shards(sources, near_tiles, far_left, far_right, pattern, band_end):
    n_col, n_row, size = near_tiles.shape[:3]
    rank = far_left.shape[2]
    cases = sources.shape[0]
    per = LANES // rank
    pairs = near_tiles.reshape(n_col // 2, 2, n_row, size, size)
    dma = pltpu.SemaphoreType.DMA
    hbm = pl.BlockSpec(memory_space=pltpu.HBM)
    smem = pl.BlockSpec(memory_space=pltpu.SMEM)
    return pl.pallas_call(
        kernel,
        out_shape=jax.ShapeDtypeStruct((cases, size), F32),
        in_specs=[hbm, hbm, hbm, hbm, smem, smem],
        out_specs=pl.BlockSpec(memory_space=pltpu.VMEM),
        scratch_shapes=[
            pltpu.VMEM(pairs.shape, BF16),
            pltpu.VMEM(pairs.shape, BF16),
            pltpu.VMEM(far_left.shape, BF16),
            pltpu.VMEM(far_right.shape, BF16),
            pltpu.VMEM((cases, size), BF16),
            pltpu.VMEM((n_col, cases, size), BF16),
            pltpu.VMEM((n_row, cases, size), BF16),
            pltpu.VMEM((n_col, n_row // per, cases, LANES), BF16),
            pltpu.VMEM((n_row, n_col // per, cases, LANES), BF16),
            pltpu.VMEM((n_col, n_row // per, 1, LANES), F32),
            pltpu.VMEM((n_row, n_col // per, 1, LANES), F32),
            pltpu.SMEM((n_col * n_row,), F32),
            pltpu.VMEM((n_col // 2, cases, size), F32),
            pltpu.VMEM((n_col // 2, cases, size), F32),
            pltpu.VMEM((n_col // 2, cases, size), BF16),
            pltpu.VMEM((n_col // 2, cases, size), BF16),
            pltpu.VMEM((n_row, cases, size), BF16),
            pltpu.VMEM((n_row, cases, size), BF16),
            pltpu.SemaphoreType.REGULAR,
            pltpu.SemaphoreType.REGULAR,
            dma,
            dma((2, 2)),
            dma((2,)),
            dma((n_col - 1,)), dma((n_col,)),
            dma((n_row,)), dma((n_row,)),
            dma((n_col // 2,)), dma((n_col // 2,)),
            dma((n_col // 2,)), dma((n_col // 2,)),
            dma((n_row,)), dma((n_row,)),
        ],
        compiler_params=pltpu.CompilerParams(
            collective_id=0, has_side_effects=True, vmem_limit_bytes=60 * 1024 * 1024
        ),
        name="panels",
    )(sources, pairs, far_left, far_right, pattern.T, band_end)


def solution(mesh):
    placed = (
        P(None, ("row", "col")),
        P("row", "col", None, None),
        P("row", "col", None, None),
        P("row", "col", None, None),
        P("row", "col"),
        P("row"),
    )
    return jax.shard_map(
        shards, mesh=mesh, in_specs=placed, out_specs=P(None, ("row", "col")), check_vma=False
    )
```

```python
import functools

import jax
import jax.numpy as jnp
from jax import lax
from jax.experimental import pallas as pl
from jax.experimental.pallas import tpu as pltpu
from jax.sharding import PartitionSpec as P

MESH = pl.DeviceIdType.MESH
F32 = jnp.float32
BF16 = jnp.bfloat16
LANES = 128


def dot_nt(a, b):
    return lax.dot_general(a, b, (((1,), (1,)), ((), ())), preferred_element_type=F32)


def dot_nn(a, b):
    return lax.dot_general(a, b, (((1,), (0,)), ((), ())), preferred_element_type=F32)


def kernel(
    src_hbm, near_hbm, left_hbm, right_hbm, pat_ref, band_ref, out_ref,
    tiles, turned, left, right, own, row_src, col_src, fwd, bwd, fwd_keep, bwd_keep, near_keep,
    pair_send, pair_recv, row_send, row_recv, col_send, col_recv,
    row_open, col_open, own_sem, near_sem, far_sem, gr_send, gr_recv, gc_send, gc_recv,
    pa_send, pa_recv, rr_send, rr_recv, rc_send, rc_recv,
):
    n_row, n_col = near_hbm.shape[2], 2 * near_hbm.shape[0]
    rank = left_hbm.shape[2]
    num_cases, size = own.shape
    per = LANES // rank
    chips = n_col // 2
    planes = n_col // 4
    row, col = lax.axis_index("row"), lax.axis_index("col")
    core, chip = lax.rem(col, 2), col // 2
    partner = col + 1 - 2 * core

    def other(c, d):
        return lax.rem(c + 2 * d, n_col)

    own_copy = pltpu.make_async_copy(src_hbm, own, own_sem)
    own_copy.start()

    barrier = pltpu.get_barrier_semaphore()

    def greet(device):
        pl.semaphore_signal(barrier, inc=1, device_id=device, device_id_type=MESH)

    @pl.loop(row + 1, n_row)
    def _(k):
        greet({"row": k, "col": col - core})

    @pl.when(core == 1)
    def _():
        greet({"col": partner})

    for d in range(1, chips):
        greet({"col": other(col - core + 1, d)})

    right_copy = pltpu.make_async_copy(right_hbm, right, far_sem.at[0])
    left_copy = pltpu.make_async_copy(left_hbm, left, far_sem.at[1])

    quarter = chips // 2

    def near_copy(side, part):
        span = pl.ds(part * quarter, quarter)
        return pltpu.make_async_copy(
            near_hbm.at[span, side], tiles.at[span, side], near_sem.at[side, part]
        )

    def theirs(t):
        return 2 * t + 1 - core

    def ours(s):
        q = s // 2
        dz = jnp.where(q == 0, 2, jnp.where(q == 1, 1, jnp.where(q == 2, 3, 0)))
        dy = 1 - lax.rem(s, 2)
        z, y = chip // 2, lax.rem(chip, 2)
        return lax.rem(z + dz, planes) * 2 + lax.rem(y + dy, 2)

    first = 1 - core
    for side in (first, core):
        for part in range(2):
            near_copy(side, part).start()
            if side is first and part == 0:
                right_copy.start()
                left_copy.start()

    @pl.when(core == 0)
    def _():
        pl.semaphore_wait(barrier, 2 * row + 1)
        pl.semaphore_signal(row_open, inc=1, device_id={"col": partner}, device_id_type=MESH)

    @pl.when(core == 1)
    def _():
        pl.semaphore_wait(row_open, 1)

    def to_row(k, src, dst, send, recv):
        return pltpu.make_async_remote_copy(
            src_ref=src, dst_ref=dst, send_sem=send, recv_sem=recv,
            device_id={"row": k}, device_id_type=MESH,
        )

    def to_col(c, src, dst, send, recv):
        return pltpu.make_async_remote_copy(
            src_ref=src, dst_ref=dst, send_sem=send, recv_sem=recv,
            device_id={"col": c}, device_id_type=MESH,
        )

    def give(block, origin, device, slot):
        return to_col(device, block, row_src.at[origin], gr_send.at[slot], gr_recv.at[origin])

    def got(origin):
        give(own, origin, partner, 0).wait_recv()

    own_copy.wait()

    @pl.loop(0, row)
    def _(k):
        to_row(k, own, col_src.at[row], gc_send.at[k], gc_recv.at[row]).start()

    give(own, col, partner, 0).start()

    col_src[row] = own[...]
    row_src[col] = own[...]

    @pl.loop(0, row)
    def _(k):
        col_src[k] = jnp.zeros_like(own)

    def weight(i, k, kind):
        big_i, big_j = row * n_col + i, k * n_col + col
        ok = (big_i <= big_j) & (big_j <= band_ref[i]) & (pat_ref[k, i] == kind)
        return jnp.where(ok, 1.0, 0.0).astype(F32)

    lane = lax.broadcasted_iota(jnp.int32, (1, LANES), 1) // rank
    wide_lane = lax.broadcasted_iota(jnp.int32, (num_cases, LANES), 1) // rank

    def lay(parts, place):
        total = parts[-1]
        for p in range(per - 1):
            total = jnp.where(place == p, parts[p], total)
        return total

    @pl.loop(0, n_col // per)
    def _(g):
        for kk in range(n_row // per):
            far = {}
            for t in range(per):
                for s in range(per):
                    i, k = g * per + t, kk * per + s
                    far[t, s] = jnp.full((1, LANES), weight(i, k, 2), F32)
                    near_keep[i * n_row + k] = weight(i, k, 1)
            for t in range(per):
                fwd_keep[g * per + t, kk] = lay([far[t, (p - t) % per] for p in range(per)], lane)
            for s in range(per):
                bwd_keep[kk * per + s, g] = lay([far[(p - s) % per, s] for p in range(per)], lane)

    def turn(t, side):
        for k in range(n_row):
            turned[t, side, k] = tiles[t, side, k].T

    near_copy(1 - core, 0).wait()

    @pl.loop(0, quarter)
    def _(t):
        turn(t, 1 - core)

    @pl.when(core == 1)
    def _():
        pl.semaphore_wait(barrier, 2 * (chips - 1))
        pl.semaphore_signal(col_open, inc=1, device_id={"col": partner}, device_id_type=MESH)

    @pl.when(core == 0)
    def _():
        pl.semaphore_wait(col_open, 1)

    @pl.loop(1, chips)
    def _(d):
        give(own, col, other(col, d), d).start()
        give(own, col, other(partner, d), chips - 1 + d).start()

    for part in range(1, 2):
        near_copy(1 - core, part).wait()

        @pl.loop(part * quarter, (part + 1) * quarter)
        def _(t):
            turn(t, 1 - core)

    for part in range(2):
        near_copy(core, part).wait()

    @pl.loop(0, quarter)
    def _(s):
        turn(ours(s), core)

    @pl.loop(row + 1, n_row)
    def _(k):
        to_row(row, own, col_src.at[k], gc_send.at[row], gc_recv.at[k]).wait_recv()

    right_copy.wait()
    left_copy.wait()
    for kk in range(n_row // per):
        for gp in range(n_col // per // 2):
            coef = []
            for s in range(per):
                k = kk * per + s
                rows = [
                    right[(gp * 2 + g) * per + (p - s) % per, k] for g in range(2) for p in range(per)
                ]
                coef.append(dot_nt(col_src[k], jnp.concatenate(rows, axis=0)))
            for g in range(2):
                for t in range(per):
                    i = (gp * 2 + g) * per + t
                    piece = lay(
                        [coef[(p - t) % per][:, g * LANES:(g + 1) * LANES] for p in range(per)],
                        wide_lane,
                    )
                    fwd[i, kk] = (piece * fwd_keep[i, kk]).astype(BF16)


    def left_rows(i):
        return jnp.concatenate(
            [
                left[i, kk * per + lax.rem(p - i + n_col, per)]
                for kk in range(n_row // per)
                for p in range(per)
            ],
            axis=0,
        )

    def row_term(i):
        acc = dot_nn(
            jnp.concatenate([fwd[i, kk] for kk in range(n_row // per)], axis=1), left_rows(i)
        )
        for k in range(n_row):
            acc += dot_nn(col_src[k] * near_keep[i * n_row + k].astype(BF16), turned[i // 2, lax.rem(i, 2), k])
        return acc

    def pair_copy(t):
        return to_col(partner, pair_send.at[t], pair_recv.at[t], pa_send.at[t], pa_recv.at[t])

    def row_copy(t):
        return to_col(
            2 * t + core, row_send.at[t], row_recv.at[chip], rr_send.at[t], rr_recv.at[chip]
        )

    def pass_on(h):
        terms = [row_term(theirs(2 * h + u)) for u in range(2)]
        turn(ours(quarter + h), core)
        for u in range(2):
            pair_send[2 * h + u] = terms[u]
        for u in range(2):
            pair_copy(2 * h + u).start()

    pass_on(0)
    pl.loop(1, chips // 2)(pass_on)

    @pl.loop(0, chips // 2)
    def _(h):
        terms = [row_term(2 * ours(2 * h + u) + core) for u in range(2)]
        for u in range(2):
            t = ours(2 * h + u)
            pair_copy(t).wait_recv()
            acc = terms[u] + pair_recv[t]

            @pl.when(t == chip)
            def _():
                out_ref[...] = acc

            @pl.when(t != chip)
            def _():
                row_send[t] = acc.astype(BF16)
                row_copy(t).start()

    @pl.loop(0, chips)
    def _(d):
        got(other(partner, d))

    @pl.loop(1, chips)
    def _(d):
        got(other(col, d))

    for g in range(n_col // per):
        back = [dot_nt(row_src[g * per + t], left_rows(g * per + t)) for t in range(per)]
        for kk in range(n_row // per):
            for s in range(per):
                k = kk * per + s
                piece = lay(
                    [back[(p - s) % per][:, kk * LANES:(kk + 1) * LANES] for p in range(per)],
                    wide_lane,
                )
                bwd[k, g] = (piece * bwd_keep[k, g]).astype(BF16)

    def col_copy(k):
        return to_row(k, col_send.at[k], col_recv.at[row], rc_send.at[k], rc_recv.at[row])

    def col_term(k):
        acc = jnp.zeros((num_cases, size), F32)
        for h in range(n_col // per // 2):
            rows = [
                right[(h * 2 + g) * per + lax.rem(p - k + n_row, per), k]
                for g in range(2)
                for p in range(per)
            ]
            acc += dot_nn(
                jnp.concatenate([bwd[k, h * 2], bwd[k, h * 2 + 1]], axis=1),
                jnp.concatenate(rows, axis=0),
            )
        for i in range(n_col):
            acc += dot_nn(row_src[i] * near_keep[i * n_row + k].astype(BF16), tiles[i // 2, i % 2, k])
        return acc

    def col_pair(high):
        terms = [col_term(high - u) for u in range(2)]
        for u in range(2):
            k, acc = high - u, terms[u]

            @pl.when(k == row)
            def _():
                out_ref[...] += acc

            @pl.when(k > row)
            def _():
                col_send[k] = acc.astype(BF16)
                col_copy(k).start()

    col_pair(n_row - 1)

    @pl.loop(1, n_row // 2)
    def _(step):
        high = n_row - 1 - 2 * step

        @pl.when(high >= row)
        def _():
            col_pair(high)

    @pl.loop(1, chips)
    def _(d):
        t = lax.rem(chip + d, chips)
        to_col(col, own, row_recv.at[t], rr_send.at[chip], rr_recv.at[t]).wait_recv()
        out_ref[...] += row_recv[t].astype(F32)

    @pl.loop(0, row)
    def _(k):
        last = row - 1 - k
        to_row(row, own, col_recv.at[last], rc_send.at[row], rc_recv.at[last]).wait_recv()
        out_ref[...] += col_recv[last].astype(F32)

    @pl.loop(0, n_col - 1)
    def _(slot):
        give(own, col, partner, slot).wait_send()

    @pl.loop(0, chips)
    def _(t):
        pair_copy(t).wait_send()

    @pl.loop(1, chips)
    def _(d):
        row_copy(lax.rem(chip + d, chips)).wait_send()

    @pl.loop(0, row)
    def _(k):
        to_row(k, own, col_src.at[row], gc_send.at[k], gc_recv.at[row]).wait_send()

    @pl.loop(row + 1, n_row)
    def _(k):
        col_copy(k).wait_send()


def shards(sources, near_tiles, far_left, far_right, pattern, band_end):
    n_col, n_row, size = near_tiles.shape[:3]
    rank = far_left.shape[2]
    cases = sources.shape[0]
    per = LANES // rank
    pairs = near_tiles.reshape(n_col // 2, 2, n_row, size, size)
    dma = pltpu.SemaphoreType.DMA
    hbm = pl.BlockSpec(memory_space=pltpu.HBM)
    smem = pl.BlockSpec(memory_space=pltpu.SMEM)
    return pl.pallas_call(
        kernel,
        out_shape=jax.ShapeDtypeStruct((cases, size), F32),
        in_specs=[hbm, hbm, hbm, hbm, smem, smem],
        out_specs=pl.BlockSpec(memory_space=pltpu.VMEM),
        scratch_shapes=[
            pltpu.VMEM(pairs.shape, BF16),
            pltpu.VMEM(pairs.shape, BF16),
            pltpu.VMEM(far_left.shape, BF16),
            pltpu.VMEM(far_right.shape, BF16),
            pltpu.VMEM((cases, size), BF16),
            pltpu.VMEM((n_col, cases, size), BF16),
            pltpu.VMEM((n_row, cases, size), BF16),
            pltpu.VMEM((n_col, n_row // per, cases, LANES), BF16),
            pltpu.VMEM((n_row, n_col // per, cases, LANES), BF16),
            pltpu.VMEM((n_col, n_row // per, 1, LANES), F32),
            pltpu.VMEM((n_row, n_col // per, 1, LANES), F32),
            pltpu.SMEM((n_col * n_row,), F32),
            pltpu.VMEM((n_col // 2, cases, size), F32),
            pltpu.VMEM((n_col // 2, cases, size), F32),
            pltpu.VMEM((n_col // 2, cases, size), BF16),
            pltpu.VMEM((n_col // 2, cases, size), BF16),
            pltpu.VMEM((n_row, cases, size), BF16),
            pltpu.VMEM((n_row, cases, size), BF16),
            pltpu.SemaphoreType.REGULAR,
            pltpu.SemaphoreType.REGULAR,
            dma,
            dma((2, 2)),
            dma((2,)),
            dma((n_col - 1,)), dma((n_col,)),
            dma((n_row,)), dma((n_row,)),
            dma((n_col // 2,)), dma((n_col // 2,)),
            dma((n_col // 2,)), dma((n_col // 2,)),
            dma((n_row,)), dma((n_row,)),
        ],
        compiler_params=pltpu.CompilerParams(
            collective_id=0, has_side_effects=True, vmem_limit_bytes=60 * 1024 * 1024
        ),
        name="panels",
    )(sources, pairs, far_left, far_right, pattern.T, band_end)


def solution(mesh):
    placed = (
        P(None, ("row", "col")),
        P("row", "col", None, None),
        P("row", "col", None, None),
        P("row", "col", None, None),
        P("row", "col"),
        P("row"),
    )
    return jax.shard_map(
        shards, mesh=mesh, in_specs=placed, out_specs=P(None, ("row", "col")), check_vma=False
    )
```

```python
import functools

import jax
import jax.numpy as jnp
from jax import lax
from jax.experimental import pallas as pl
from jax.experimental.pallas import tpu as pltpu
from jax.sharding import PartitionSpec as P

MESH = pl.DeviceIdType.MESH
F32 = jnp.float32
BF16 = jnp.bfloat16
LANES = 128


def dot_nt(a, b):
    return lax.dot_general(a, b, (((1,), (1,)), ((), ())), preferred_element_type=F32)


def dot_nn(a, b):
    return lax.dot_general(a, b, (((1,), (0,)), ((), ())), preferred_element_type=F32)


def kernel(
    src_hbm, near_hbm, left_hbm, right_hbm, pat_ref, band_ref, out_ref,
    tiles, turned, left, right, own, row_src, col_src, fwd, bwd, fwd_keep, bwd_keep, near_keep,
    pair_send, pair_recv, row_send, row_recv, col_send, col_recv,
    row_open, col_open, own_sem, near_sem, far_sem, gr_send, gr_recv, gc_send, gc_recv,
    pa_send, pa_recv, rr_send, rr_recv, rc_send, rc_recv,
):
    n_row, n_col = near_hbm.shape[2], 2 * near_hbm.shape[0]
    rank = left_hbm.shape[2]
    num_cases, size = own.shape
    per = LANES // rank
    chips = n_col // 2
    planes = n_col // 4
    row, col = lax.axis_index("row"), lax.axis_index("col")
    core, chip = lax.rem(col, 2), col // 2
    partner = col + 1 - 2 * core

    def other(c, d):
        return lax.rem(c + 2 * d, n_col)

    own_copy = pltpu.make_async_copy(src_hbm, own, own_sem)
    own_copy.start()

    barrier = pltpu.get_barrier_semaphore()

    def greet(device):
        pl.semaphore_signal(barrier, inc=1, device_id=device, device_id_type=MESH)

    @pl.loop(row + 1, n_row)
    def _(k):
        greet({"row": k, "col": col - core})

    @pl.when(core == 1)
    def _():
        greet({"col": partner})

    for d in range(1, chips):
        greet({"col": other(col - core + 1, d)})

    right_copy = pltpu.make_async_copy(right_hbm, right, far_sem.at[0])
    left_copy = pltpu.make_async_copy(left_hbm, left, far_sem.at[1])

    quarter = chips // 2

    def near_copy(side, part):
        span = pl.ds(part * quarter, quarter)
        return pltpu.make_async_copy(
            near_hbm.at[span, side], tiles.at[span, side], near_sem.at[side, part]
        )

    def theirs(t):
        return 2 * t + 1 - core

    def ours(s):
        q = s // 2
        dz = jnp.where(q == 0, 2, jnp.where(q == 1, 1, jnp.where(q == 2, 3, 0)))
        dy = 1 - lax.rem(s, 2)
        z, y = chip // 2, lax.rem(chip, 2)
        return lax.rem(z + dz, planes) * 2 + lax.rem(y + dy, 2)

    first = 1 - core
    for side in (first, core):
        for part in range(2):
            near_copy(side, part).start()
    right_copy.start()
    left_copy.start()

    @pl.when(core == 0)
    def _():
        pl.semaphore_wait(barrier, 2 * row + 1)
        pl.semaphore_signal(row_open, inc=1, device_id={"col": partner}, device_id_type=MESH)

    @pl.when(core == 1)
    def _():
        pl.semaphore_wait(row_open, 1)

    def to_row(k, src, dst, send, recv):
        return pltpu.make_async_remote_copy(
            src_ref=src, dst_ref=dst, send_sem=send, recv_sem=recv,
            device_id={"row": k}, device_id_type=MESH,
        )

    def to_col(c, src, dst, send, recv):
        return pltpu.make_async_remote_copy(
            src_ref=src, dst_ref=dst, send_sem=send, recv_sem=recv,
            device_id={"col": c}, device_id_type=MESH,
        )

    def give(block, origin, device, slot):
        return to_col(device, block, row_src.at[origin], gr_send.at[slot], gr_recv.at[origin])

    def got(origin):
        give(own, origin, partner, 0).wait_recv()

    own_copy.wait()

    @pl.loop(0, row)
    def _(k):
        to_row(k, own, col_src.at[row], gc_send.at[k], gc_recv.at[row]).start()

    give(own, col, partner, 0).start()

    col_src[row] = own[...]
    row_src[col] = own[...]

    @pl.loop(0, row)
    def _(k):
        col_src[k] = jnp.zeros_like(own)

    def weight(i, k, kind):
        big_i, big_j = row * n_col + i, k * n_col + col
        ok = (big_i <= big_j) & (big_j <= band_ref[i]) & (pat_ref[k, i] == kind)
        return jnp.where(ok, 1.0, 0.0).astype(F32)

    lane = lax.broadcasted_iota(jnp.int32, (1, LANES), 1) // rank
    wide_lane = lax.broadcasted_iota(jnp.int32, (num_cases, LANES), 1) // rank

    def lay(parts, place):
        total = parts[-1]
        for p in range(per - 1):
            total = jnp.where(place == p, parts[p], total)
        return total

    @pl.loop(0, n_col // per)
    def _(g):
        for kk in range(n_row // per):
            far = {}
            for t in range(per):
                for s in range(per):
                    i, k = g * per + t, kk * per + s
                    far[t, s] = jnp.full((1, LANES), weight(i, k, 2), F32)
                    near_keep[i * n_row + k] = weight(i, k, 1)
            for t in range(per):
                fwd_keep[g * per + t, kk] = lay([far[t, (p - t) % per] for p in range(per)], lane)
            for s in range(per):
                bwd_keep[kk * per + s, g] = lay([far[(p - s) % per, s] for p in range(per)], lane)

    def turn(t, side):
        for k in range(n_row):
            turned[t, side, k] = tiles[t, side, k].T

    near_copy(1 - core, 0).wait()

    @pl.loop(0, quarter)
    def _(t):
        turn(t, 1 - core)

    @pl.when(core == 1)
    def _():
        pl.semaphore_wait(barrier, 2 * (chips - 1))
        pl.semaphore_signal(col_open, inc=1, device_id={"col": partner}, device_id_type=MESH)

    @pl.when(core == 0)
    def _():
        pl.semaphore_wait(col_open, 1)

    @pl.loop(1, chips)
    def _(d):
        give(own, col, other(col, d), d).start()
        give(own, col, other(partner, d), chips - 1 + d).start()

    for part in range(1, 2):
        near_copy(1 - core, part).wait()

        @pl.loop(part * quarter, (part + 1) * quarter)
        def _(t):
            turn(t, 1 - core)

    for part in range(2):
        near_copy(core, part).wait()

    @pl.loop(0, quarter)
    def _(s):
        turn(ours(s), core)

    @pl.loop(row + 1, n_row)
    def _(k):
        to_row(row, own, col_src.at[k], gc_send.at[row], gc_recv.at[k]).wait_recv()

    right_copy.wait()
    left_copy.wait()
    for kk in range(n_row // per):
        for gp in range(n_col // per // 2):
            coef = []
            for s in range(per):
                k = kk * per + s
                rows = [
                    right[(gp * 2 + g) * per + (p - s) % per, k] for g in range(2) for p in range(per)
                ]
                coef.append(dot_nt(col_src[k], jnp.concatenate(rows, axis=0)))
            for g in range(2):
                for t in range(per):
                    i = (gp * 2 + g) * per + t
                    piece = lay(
                        [coef[(p - t) % per][:, g * LANES:(g + 1) * LANES] for p in range(per)],
                        wide_lane,
                    )
                    fwd[i, kk] = (piece * fwd_keep[i, kk]).astype(BF16)


    def left_rows(i):
        return jnp.concatenate(
            [
                left[i, kk * per + lax.rem(p - i + n_col, per)]
                for kk in range(n_row // per)
                for p in range(per)
            ],
            axis=0,
        )

    def row_term(i):
        acc = dot_nn(
            jnp.concatenate([fwd[i, kk] for kk in range(n_row // per)], axis=1), left_rows(i)
        )
        for k in range(n_row):
            acc += dot_nn(col_src[k] * near_keep[i * n_row + k].astype(BF16), turned[i // 2, lax.rem(i, 2), k])
        return acc

    def pair_copy(t):
        return to_col(partner, pair_send.at[t], pair_recv.at[t], pa_send.at[t], pa_recv.at[t])

    def row_copy(t):
        return to_col(
            2 * t + core, row_send.at[t], row_recv.at[chip], rr_send.at[t], rr_recv.at[chip]
        )

    def pass_on(h):
        terms = [row_term(theirs(2 * h + u)) for u in range(2)]
        turn(ours(quarter + h), core)
        for u in range(2):
            pair_send[2 * h + u] = terms[u]
        for u in range(2):
            pair_copy(2 * h + u).start()

    pass_on(0)
    pl.loop(1, chips // 2)(pass_on)

    @pl.loop(0, chips // 2)
    def _(h):
        terms = [row_term(2 * ours(2 * h + u) + core) for u in range(2)]
        for u in range(2):
            t = ours(2 * h + u)
            pair_copy(t).wait_recv()
            acc = terms[u] + pair_recv[t]

            @pl.when(t == chip)
            def _():
                out_ref[...] = acc

            @pl.when(t != chip)
            def _():
                row_send[t] = acc.astype(BF16)
                row_copy(t).start()

    @pl.loop(0, chips)
    def _(d):
        got(other(partner, d))

    @pl.loop(1, chips)
    def _(d):
        got(other(col, d))

    for g in range(n_col // per):
        back = [dot_nt(row_src[g * per + t], left_rows(g * per + t)) for t in range(per)]
        for kk in range(n_row // per):
            for s in range(per):
                k = kk * per + s
                piece = lay(
                    [back[(p - s) % per][:, kk * LANES:(kk + 1) * LANES] for p in range(per)],
                    wide_lane,
                )
                bwd[k, g] = (piece * bwd_keep[k, g]).astype(BF16)

    def col_copy(k):
        return to_row(k, col_send.at[k], col_recv.at[row], rc_send.at[k], rc_recv.at[row])

    def col_term(k):
        acc = jnp.zeros((num_cases, size), F32)
        for h in range(n_col // per // 2):
            rows = [
                right[(h * 2 + g) * per + lax.rem(p - k + n_row, per), k]
                for g in range(2)
                for p in range(per)
            ]
            acc += dot_nn(
                jnp.concatenate([bwd[k, h * 2], bwd[k, h * 2 + 1]], axis=1),
                jnp.concatenate(rows, axis=0),
            )
        for i in range(n_col):
            acc += dot_nn(row_src[i] * near_keep[i * n_row + k].astype(BF16), tiles[i // 2, i % 2, k])
        return acc

    def col_pair(high):
        terms = [col_term(high - u) for u in range(2)]
        for u in range(2):
            k, acc = high - u, terms[u]

            @pl.when(k == row)
            def _():
                out_ref[...] += acc

            @pl.when(k > row)
            def _():
                col_send[k] = acc.astype(BF16)
                col_copy(k).start()

    col_pair(n_row - 1)

    @pl.loop(1, n_row // 2)
    def _(step):
        high = n_row - 1 - 2 * step

        @pl.when(high >= row)
        def _():
            col_pair(high)

    @pl.loop(1, chips)
    def _(d):
        t = lax.rem(chip + d, chips)
        to_col(col, own, row_recv.at[t], rr_send.at[chip], rr_recv.at[t]).wait_recv()
        out_ref[...] += row_recv[t].astype(F32)

    @pl.loop(0, row)
    def _(k):
        last = row - 1 - k
        to_row(row, own, col_recv.at[last], rc_send.at[row], rc_recv.at[last]).wait_recv()
        out_ref[...] += col_recv[last].astype(F32)

    @pl.loop(0, n_col - 1)
    def _(slot):
        give(own, col, partner, slot).wait_send()

    @pl.loop(0, chips)
    def _(t):
        pair_copy(t).wait_send()

    @pl.loop(1, chips)
    def _(d):
        row_copy(lax.rem(chip + d, chips)).wait_send()

    @pl.loop(0, row)
    def _(k):
        to_row(k, own, col_src.at[row], gc_send.at[k], gc_recv.at[row]).wait_send()

    @pl.loop(row + 1, n_row)
    def _(k):
        col_copy(k).wait_send()


def shards(sources, near_tiles, far_left, far_right, pattern, band_end):
    n_col, n_row, size = near_tiles.shape[:3]
    rank = far_left.shape[2]
    cases = sources.shape[0]
    per = LANES // rank
    pairs = near_tiles.reshape(n_col // 2, 2, n_row, size, size)
    dma = pltpu.SemaphoreType.DMA
    hbm = pl.BlockSpec(memory_space=pltpu.HBM)
    smem = pl.BlockSpec(memory_space=pltpu.SMEM)
    return pl.pallas_call(
        kernel,
        out_shape=jax.ShapeDtypeStruct((cases, size), F32),
        in_specs=[hbm, hbm, hbm, hbm, smem, smem],
        out_specs=pl.BlockSpec(memory_space=pltpu.VMEM),
        scratch_shapes=[
            pltpu.VMEM(pairs.shape, BF16),
            pltpu.VMEM(pairs.shape, BF16),
            pltpu.VMEM(far_left.shape, BF16),
            pltpu.VMEM(far_right.shape, BF16),
            pltpu.VMEM((cases, size), BF16),
            pltpu.VMEM((n_col, cases, size), BF16),
            pltpu.VMEM((n_row, cases, size), BF16),
            pltpu.VMEM((n_col, n_row // per, cases, LANES), BF16),
            pltpu.VMEM((n_row, n_col // per, cases, LANES), BF16),
            pltpu.VMEM((n_col, n_row // per, 1, LANES), F32),
            pltpu.VMEM((n_row, n_col // per, 1, LANES), F32),
            pltpu.SMEM((n_col * n_row,), F32),
            pltpu.VMEM((n_col // 2, cases, size), F32),
            pltpu.VMEM((n_col // 2, cases, size), F32),
            pltpu.VMEM((n_col // 2, cases, size), BF16),
            pltpu.VMEM((n_col // 2, cases, size), BF16),
            pltpu.VMEM((n_row, cases, size), BF16),
            pltpu.VMEM((n_row, cases, size), BF16),
            pltpu.SemaphoreType.REGULAR,
            pltpu.SemaphoreType.REGULAR,
            dma,
            dma((2, 2)),
            dma((2,)),
            dma((n_col - 1,)), dma((n_col,)),
            dma((n_row,)), dma((n_row,)),
            dma((n_col // 2,)), dma((n_col // 2,)),
            dma((n_col // 2,)), dma((n_col // 2,)),
            dma((n_row,)), dma((n_row,)),
        ],
        compiler_params=pltpu.CompilerParams(
            collective_id=0, has_side_effects=True, vmem_limit_bytes=60 * 1024 * 1024
        ),
        name="panels",
    )(sources, pairs, far_left, far_right, pattern.T, band_end)


def solution(mesh):
    placed = (
        P(None, ("row", "col")),
        P("row", "col", None, None),
        P("row", "col", None, None),
        P("row", "col", None, None),
        P("row", "col"),
        P("row"),
    )
    return jax.shard_map(
        shards, mesh=mesh, in_specs=placed, out_specs=P(None, ("row", "col")), check_vma=False
    )
```
